1024 devices in a mesh: dp: 16 (over x, core), expert: 64 (over z, y).
Axes of the slice: x: 8, y: 8, z: 8, core: 2. Of those that a mesh axis runs over, the one named last changes fastest.
Arguments:
- tokens: bfloat16 [12288, 4096], P('expert', 'dp'), may hold values from -6 to 6
- routes: int32 [12288, 2], P('expert'), may hold values from 0 to 63, all different within a row; in each aligned block of 192 rows (0 to 191, 192 to 383, ...) at most 7 rows name the same one
- route_weight: float32 [12288, 2], P('expert'), may hold values from 0.2 to 1
- cotangent: bfloat16 [12288, 4096], P('expert', 'dp'), may hold values from -4 to 4
- w_in: bfloat16 [64, 4096, 2048], P('expert', 'dp'), may hold values from -0.09375 to 0.09375
- w_out: bfloat16 [64, 1024, 4096], P('expert', None, 'dp'), may hold values from -0.1875 to 0.1875
Outputs:
- mixed: bfloat16 [12288, 4096], P('expert', 'dp')
- grad_tokens: bfloat16 [12288, 4096], P('expert', 'dp')
- grad_in: bfloat16 [64, 4096, 2048], P('expert', 'dp')
- grad_out: bfloat16 [64, 1024, 4096], P('expert', None, 'dp')
The draws below stay inside these ranges and needn't reach their ends.
Inputs may be any that keep to these rules, and one draw needn't show every extreme that they name: `routes`: each row names 2 different experts. Among the 192 rows of one index of the expert axis no expert is named more than 7 times, and in every draw some expert is named exactly 7 times by such a block.
All inputs are finite; a program needn't handle non-finite values.
Results may differ from the reference program's by a relative error of at most 0.0065.
Values may be sent and summed in bfloat16 or wider, within the bound.
A program may use at most 64 MiB of HBM per device.

```python
import math
import jax
import jax.numpy as jnp
import numpy as np
from jax import lax

D = 4096
FF = 1024
TOK_DEV = 192
TOPK = 2
EXPERTS = 64
TOKENS = 12288
CAP = 7
N_EXPERT = 64


def block_levels(key, extent, shards, least, top_value):
    loudness, own = 1.0, jax.random.fold_in(key, 6)
    for position, blocks in shards:
        draws = jnp.exp(jax.random.uniform(jax.random.fold_in(own, position), (blocks,), jnp.float32, least / len(shards), top_value / len(shards)))
        loudness = loudness * jnp.repeat(draws, extent[position] // blocks).reshape([-1 if axis == position else 1 for axis in range(len(extent))])
    return loudness


def shared_out(rng, own, number, rows, count, top, bound, lean):
    ranking = jax.random.permutation(rng, count)
    crowded, common = portions_of(count, rows * top, bound, lean, True), portions_of(count, rows * top, bound, lean, False)
    places = jnp.arange(count)

    def named(lengths, offset_by):
        used = int((lengths > 0).sum())
        fixed = max(1, used // 4)
        moved = fixed + (places - fixed + offset_by * (used - fixed)) % max(1, count - fixed)
        return jnp.zeros((count,), jnp.int32).at[ranking[jnp.where(places < fixed, places, moved)]].set(jnp.asarray(lengths, jnp.int32))

    lengths = jnp.where(number % 4 == 0, named(crowded, number // 4), named(common, number - number // 4 - 1))
    mixed = jax.random.permutation(jax.random.fold_in(own, 3), count)
    giver, receiver = mixed[0:count // 2 * 2:2], mixed[1:count // 2 * 2:2]
    room = jnp.minimum(lengths[giver] - 1, bound - lengths[receiver]) // 2
    room = jnp.where((giver == ranking[0]) | (receiver == ranking[0]) | (lengths[receiver] == 0), 0, jnp.maximum(room, 0))
    moved = jax.random.randint(jax.random.fold_in(own, 4), (count // 2,), 0, 1 << 20) % (room + 1)
    lengths = lengths.at[giver].add(-moved).at[receiver].add(moved)
    items = jnp.searchsorted(jnp.cumsum(lengths), jnp.arange(rows * top), side="right").astype(jnp.int32)
    table = items.reshape(top, rows).T
    table = table[jax.random.permutation(jax.random.fold_in(own, 1), rows)]
    offset_by = jax.random.randint(jax.random.fold_in(own, 2), (rows, 1), 0, top)
    return jnp.take_along_axis(table, (jnp.arange(top)[None, :] + offset_by) % top, axis=1)


def portions_of(count, total, most, slope, full):
    portions = [(1 << 20) // math.isqrt(standing ** slope) + 1 for standing in range(1, count + 1)]
    largest = most if full else min(most, max(-(-total // count), total * portions[0] // sum(portions)))
    least = 1 if total - largest >= count - 1 else 0
    given, rest = [largest] + [least] * (count - 1), total - largest - least * (count - 1)
    while rest > 0:
        movable = [i for i in range(1, count) if given[i] < largest] or [i for i in range(1, count) if given[i] < most]
        pool, left = sum([portions[i] for i in movable]), rest
        for i in movable:
            extra = min(most - given[i], max(1, left * portions[i] // pool), rest)
            given[i] = given[i] + extra
            rest = rest - extra
    return np.array(given)


def centred(stream_key, shape, scale, reach, shards=(), held_as=jnp.bfloat16):
    result = jax.random.normal(stream_key, shape, jnp.float32) * scale
    if len(shards) > 0:
        result = block_levels(stream_key, shape, shards, -0.22, 0.18) * result
    return jnp.clip(result, min=-reach, max=reach).astype(held_as)


def setup_inputs(seed: int = 0) -> dict:
    seeds = jax.random.split(jax.random.key(seed), 7)
    tokens = centred(seeds[0], (TOKENS, D), 1.0, 6.0, ((0, 64), (1, 16)))
    routes_keys = jax.random.split(jax.random.fold_in(seeds[1], 1), TOKENS // TOK_DEV)
    routes_turns = jax.random.permutation(jax.random.fold_in(seeds[1], 3), TOKENS // TOK_DEV)
    routes = jax.vmap(lambda own, number: shared_out(jax.random.fold_in(seeds[1], 2), own, number, TOK_DEV, EXPERTS, TOPK, CAP, 2))(routes_keys, routes_turns).reshape((TOKENS, TOPK))
    route_weight = jnp.clip(0.2 + 0.8 * jax.random.uniform(seeds[2], (TOKENS, TOPK), jnp.float32) ** block_levels(seeds[2], (TOKENS, TOPK), ((0, 64),), -0.2, 0.2), 0.2, 1.0)
    cotangent = centred(seeds[3], (TOKENS, D), 0.25, 4.0, ((0, 64), (1, 16)))
    w_in = centred(seeds[4], (EXPERTS, D, 2 * FF), D ** -0.5, 0.09375, ((0, 64), (1, 16)))
    w_out = centred(seeds[5], (EXPERTS, FF, D), FF ** -0.5, 0.1875, ((0, 64), (2, 16)))
    return {"tokens": tokens, "routes": routes, "route_weight": route_weight, "cotangent": cotangent, "w_in": w_in, "w_out": w_out}


def slot_ranks(routes):
    blocks = routes.reshape(N_EXPERT, TOK_DEV * TOPK)
    onehot = (blocks[:, :, None] == jnp.arange(EXPERTS, dtype=jnp.int32)[None, None, :]).astype(jnp.int32)
    before = jnp.cumsum(onehot, axis=1) - onehot
    return jnp.sum(before * onehot, axis=-1).astype(jnp.int32)


def activate(pre_act, grad_hidden):
    gate_part = pre_act[:, :FF]
    up_part = pre_act[:, FF:]
    sigmoid_gate = jax.nn.sigmoid(gate_part)
    silu_gate = gate_part * sigmoid_gate
    hidden = (silu_gate * up_part).astype(jnp.bfloat16)
    grad_gate = grad_hidden * up_part * sigmoid_gate * (1.0 + gate_part * (1.0 - sigmoid_gate))
    grad_up = grad_hidden * silu_gate
    return hidden, jnp.concatenate([grad_gate, grad_up], axis=1).astype(jnp.bfloat16)


def expert_pass(routed_rows, routed_grads, w_in_one, w_out_one):
    pre_act = jnp.dot(routed_rows, w_in_one, preferred_element_type=jnp.float32)
    grad_hidden = jnp.dot(routed_grads, w_out_one.T, preferred_element_type=jnp.float32)
    hidden, grad_both = activate(pre_act, grad_hidden)
    out_rows = jnp.dot(hidden, w_out_one, preferred_element_type=jnp.float32).astype(jnp.bfloat16)
    grad_rows = jnp.dot(grad_both, w_in_one.T, preferred_element_type=jnp.float32).astype(jnp.bfloat16)
    grad_in_one = jnp.dot(routed_rows.T, grad_both, preferred_element_type=jnp.float32).astype(jnp.bfloat16)
    grad_out_one = jnp.dot(hidden.T, routed_grads, preferred_element_type=jnp.float32).astype(jnp.bfloat16)
    return out_rows, grad_rows, grad_in_one, grad_out_one


def reference(tokens, routes, route_weight, cotangent, w_in, w_out):
    slot_rank = slot_ranks(routes).reshape(TOKENS, TOPK)
    token_ids = jnp.broadcast_to(jnp.arange(TOKENS, dtype=jnp.int32)[:, None], (TOKENS, TOPK))
    source_dev = (token_ids // TOK_DEV).astype(jnp.int32)
    slot_place = ((routes * N_EXPERT + source_dev) * CAP + slot_rank).astype(jnp.int32)
    slot_count = EXPERTS * N_EXPERT * CAP
    slot_token = jnp.full((slot_count,), TOKENS, jnp.int32).at[slot_place.reshape(-1)].set(token_ids.reshape(-1))
    slot_weight = jnp.zeros((slot_count,), jnp.float32).at[slot_place.reshape(-1)].set(route_weight.reshape(-1))
    tokens_padded = jnp.concatenate([tokens, jnp.zeros((1, D), tokens.dtype)], axis=0)
    cotangent_padded = jnp.concatenate([cotangent, jnp.zeros((1, D), cotangent.dtype)], axis=0)
    per_slots = N_EXPERT * CAP

    def per_expert(inputs):
        expert_id, w_in_one, w_out_one = inputs
        row_index = lax.dynamic_slice_in_dim(slot_token, (expert_id * per_slots).astype(jnp.int32), per_slots)
        row_weight = lax.dynamic_slice_in_dim(slot_weight, (expert_id * per_slots).astype(jnp.int32), per_slots)
        routed_rows = tokens_padded[row_index]
        routed_grads = (row_weight[:, None] * cotangent_padded[row_index].astype(jnp.float32)).astype(jnp.bfloat16)
        return expert_pass(routed_rows, routed_grads, w_in_one, w_out_one)

    out_rows, grad_rows, grad_in, grad_out = lax.map(per_expert, (jnp.arange(EXPERTS, dtype=jnp.int32), w_in, w_out))
    route_out = out_rows.reshape(slot_count, D)[slot_place].astype(jnp.float32)
    mixed = jnp.sum(route_weight[:, :, None] * route_out, axis=1).astype(jnp.bfloat16)
    route_grad = grad_rows.reshape(slot_count, D)[slot_place].astype(jnp.float32)
    grad_tokens = jnp.sum(route_grad, axis=1).astype(jnp.bfloat16)
    return mixed, grad_tokens, grad_in, grad_out
```

```python
import functools
import math

import jax
import jax.numpy as jnp
from jax import lax
from jax.experimental import pallas as pl
from jax.experimental.pallas import tpu as pltpu
from jax.sharding import PartitionSpec as P

BF = jnp.bfloat16
F32 = jnp.float32
MESH = pl.DeviceIdType.MESH
BLOCK = 16


def dot(a, b, dims=((1,), (0,))):
    return lax.dot_general(a, b, (dims, ((), ())), preferred_element_type=F32)


def ones_where(mask):
    return jnp.where(mask, 1.0, 0.0).astype(BF)


def iota(shape, dim):
    return lax.broadcasted_iota(jnp.int32, shape, dim)


def kernel(
    NX, NZ, NY, CAP,
    routes, weights, tokens, cot, w_in, w_out,
    mixed, grad_tokens, grad_in, grad_out,
    wi, wo, sa, sb, r1a, r1b, r2a, r2b, x, xp, pp, rsend, rrecv, g, acc, qmat, wcol,
    wsend, wrecv, wlocal, asend, arecv, alocal, xsend, xrecv, rs_s, rs_r, ag_s, ag_r, d_s, d_r,
):
    T, F = tokens.shape
    U = w_out.shape[0]
    E = NZ * NY
    UB = U // NX
    R = E * CAP
    HR = R // 2
    QR = R // 4
    K = NX // 2
    EG = E // 4
    HF = F // 2

    me_dp = lax.axis_index("dp")
    me_e = lax.axis_index("expert")
    xc, core = me_dp // 2, me_dp % 2
    Z, Y = me_e // NY, me_e % NY
    right = {"dp": ((xc + 1) % NX) * 2 + core, "expert": me_e}
    left = {"dp": ((xc + NX - 1) % NX) * 2 + core, "expert": me_e}
    partner = {"dp": xc * 2 + (1 - core), "expert": me_e}

    def z_peer(d):
        zz = (Z + d) % NZ
        return zz, {"dp": me_dp, "expert": zz * NY + Y}

    def y_peer(d):
        yy = (Y + d) % NY
        return yy, {"dp": me_dp, "expert": Z * NY + yy}

    def remote(src, dst, send, recv, device):
        return pltpu.make_async_remote_copy(
            src_ref=src, dst_ref=dst, send_sem=send, recv_sem=recv,
            device_id=device, device_id_type=MESH,
        )

    barrier = pltpu.get_barrier_semaphore()
    for d in range(1, NZ):
        pl.semaphore_signal(barrier, inc=1, device_id=z_peer(d)[1], device_id_type=MESH)
    for d in range(1, NY):
        pl.semaphore_signal(barrier, inc=1, device_id=y_peer(d)[1], device_id_type=MESH)
    for device in (right, left, partner):
        pl.semaphore_signal(barrier, inc=1, device_id=device, device_id_type=MESH)

    local_w = [
        pltpu.make_async_copy(w_in, wi.at[0], wlocal.at[0]),
        pltpu.make_async_copy(w_out, wo.at[0], wlocal.at[1]),
    ]
    for copy in local_w:
        copy.start()

    upper = ones_where(iota((T, T), 0) < iota((T, T), 1))
    diagonal = iota((T, T), 0) == iota((T, T), 1)
    named = [iota((E, T), 0) == routes[k : k + 1, :] for k in range(2)]
    before = dot(ones_where(named[0] | named[1]), upper)
    rows_of, cols_of, scaled, wcols = [], [], [], []
    cot_f = cot[...].astype(F32)
    for k in range(2):
        rank = jnp.sum(jnp.where(named[k], before, 0.0), axis=0, keepdims=True)
        place = routes[k : k + 1, :].astype(F32) * float(BLOCK) + rank
        col = jnp.sum(jnp.where(diagonal, place, 0.0), axis=1, keepdims=True)
        wc = jnp.sum(jnp.where(diagonal, weights[k : k + 1, :], 0.0), axis=1, keepdims=True)
        rows_of.append(place.astype(jnp.int32))
        cols_of.append(col.astype(jnp.int32))
        wcols.append(wc)
        scaled.append((wc * cot_f).astype(BF))
    token_rows = tokens[...]
    for i in range(4):
        ri = iota((EG * BLOCK, T), 0) + i * EG * BLOCK
        block = dot(ones_where((ri == rows_of[0]) | (ri == rows_of[1])), token_rows)
        for k in range(2):
            block += dot(ones_where(ri == rows_of[k] + 8), scaled[k])
        block = block.astype(BF)
        sa[0, i] = block[:, :HF]
        sb[0, i] = block[:, HF:]

    pl.semaphore_wait(barrier, NZ + NY + 1)

    def p1a(q, d):
        zz, device = z_peer(d)
        return remote(sa4(q, zz), r1a.at[q, Z], asend.at[q, 0, d], arecv.at[q, 0, d], device)

    def p1b(q, d):
        yy, device = y_peer(d)
        return remote(sb4(q, yy), r1b.at[q, Y], asend.at[q, 1, d], arecv.at[q, 1, d], device)

    def p2a(q, d):
        yy, device = y_peer(d)
        return remote(r1a.at[q, :, yy], r2a.at[q, :, Y], asend.at[q, 2, d], arecv.at[q, 2, d], device)

    def p2b(q, d):
        zz, device = z_peer(d)
        return remote(r1b.at[q, :, zz], r2b.at[q, Z], asend.at[q, 3, d], arecv.at[q, 3, d], device)

    def sa4(q, zz):
        return s4a.at[q, zz]

    def sb4(q, yy):
        return s4b.at[q, :, yy]

    s4a = sa.reshape(2, NZ, NY, BLOCK, HF)
    s4b = sb.reshape(2, NZ, NY, BLOCK, HF)

    def local(q, i):
        src, dst = (
            (sa4(q, Z), r1a.at[q, Z]),
            (sb4(q, Y), r1b.at[q, Y]),
            (r1a.at[q, :, Y], r2a.at[q, :, Y]),
            (r1b.at[q, :, Z], r2b.at[q, Z]),
        )[i]
        return pltpu.make_async_copy(src, dst, alocal.at[q, i])

    def order(n):
        ds = []
        for hop in range(n // 2, 0, -1):
            ds += [hop] if 2 * hop == n else [hop, n - hop]
        return ds

    def phase_one(q):
        for i in range(max(NZ, NY)):
            if i < len(order(NZ)):
                p1a(q, order(NZ)[i]).start()
            if i < len(order(NY)):
                p1b(q, order(NY)[i]).start()
        local(q, 0).start()
        local(q, 1).start()

    def phase_two(q):
        local(q, 0).wait()
        for d in order(NZ):
            p1a(q, d).wait_recv()
        for d in order(NY):
            p2a(q, d).start()
        local(q, 2).start()
        local(q, 1).wait()
        for d in order(NY):
            p1b(q, d).wait_recv()
        for d in order(NZ):
            p2b(q, d).start()
        local(q, 3).start()

    def phase_end(q):
        local(q, 2).wait()
        local(q, 3).wait()
        for d in order(NY):
            p2a(q, d).wait_recv()
        for d in order(NZ):
            p2b(q, d).wait_recv()

    phase_one(0)
    give_w = [
        remote(w_in, wi.at[1], wsend.at[0], wrecv.at[0], partner),
        remote(w_out, wo.at[1], wsend.at[1], wrecv.at[1], partner),
    ]
    for copy in give_w:
        copy.start()

    ci = iota((T, E * BLOCK), 1)
    for k in range(2):
        qmat[k] = ones_where(ci == cols_of[k])
        wcol[k] = jnp.broadcast_to(wcols[k], (T, F))
    qmat[2] = ones_where((ci == cols_of[0] + 8) | (ci == cols_of[1] + 8))

    phase_two(0)

    bj = iota((1, EG * BLOCK), 1)
    src, j = bj // BLOCK, bj % BLOCK
    pick = []
    for offset in (0, 8):
        ok = (j >= offset) & (j < offset + CAP)
        pick.append(jnp.where(ok, src * CAP + j - offset, -1))
    want = iota((QR, EG * BLOCK), 0)
    unpack = [ones_where(want == pick[a]) for a in range(2)]

    phase_end(0)
    for i in range(4):
        lo, hi = i * EG, (i + 1) * EG
        half_a = r2a[0].reshape(E, BLOCK, HF)[lo:hi].reshape(EG * BLOCK, HF)
        half_b = r2b[0].reshape(E, BLOCK, HF)[lo:hi].reshape(EG * BLOCK, HF)
        for a in range(2):
            x[i // 2, a, i % 2, :, :HF] = dot(unpack[a], half_a).astype(BF)
            x[i // 2, a, i % 2, :, HF:] = dot(unpack[a], half_b).astype(BF)
    give_x = remote(x.at[1 - core], xp, xsend, xrecv, partner)
    give_x.start()
    for copy in local_w:
        copy.wait()
    for copy in give_w:
        copy.wait_recv()
    give_x.wait_recv()

    def partial(jb):
        at = pl.multiple_of(jb * UB, UB)
        for n in range(3):
            total = None
            for v, rows in ((0, x.at[core]), (1, xp)):
                if n < 2:
                    lhs = rows[0].reshape(HR, F)
                    part = dot(lhs, wi[v, :, pl.ds(pl.multiple_of(n * U + at, UB), UB)])
                else:
                    lhs = rows[1].reshape(HR, F)
                    part = dot(lhs, wo[v, pl.ds(at, UB), :], ((1,), (1,)))
                total = part if total is None else total + part
            pp[jb, 0, :, n * UB : (n + 1) * UB] = total[:QR]
            pp[jb, 1, :, n * UB : (n + 1) * UB] = total[QR:]

    def chunk_of(direction, s):
        return (xc + K - s) % NX if direction == 0 else (xc + NX - K + s) % NX

    def ring(direction, s, q):
        return remote(
            rsend.at[direction, s, q], rrecv.at[direction, s, q],
            rs_s.at[direction, s, q], rs_r.at[direction, s, q],
            (right, left)[direction],
        )

    def exists(direction, s, q):
        return s > 0 or q == direction

    def ring_step(direction, s, q):
        value = pp[chunk_of(direction, s), q]
        if s > 0 and exists(direction, s - 1, q):
            ring(direction, s - 1, q).wait_recv()
            value = value + rrecv[direction, s - 1, q].astype(F32)
        rsend[direction, s, q] = value.astype(BF)
        ring(direction, s, q).start()

    partial((xc + K) % NX)
    for direction in range(2):
        ring_step(direction, 0, direction)
    if K > 1:
        partial(chunk_of(0, 1))
        ring_step(0, 1, 1)
        partial(chunk_of(1, 1))
        ring_step(1, 1, 0)

    def others(i, carry):
        partial((xc + NX - (K - 2) + i) % NX)
        return carry

    if K > 1:
        lax.fori_loop(0, 2 * (K - 2) + 1, others, 0)
    else:
        partial(xc)
    for s in range(1, K):
        for q_of in (1, 0):
            for direction in range(2):
                q = q_of if direction == 0 else 1 - q_of
                if s == 1 and q_of == 1:
                    continue
                ring_step(direction, s, q)

    def ag(direction, s, q):
        jb = (xc + NX - s) % NX if direction == 0 else (xc + s) % NX
        return remote(
            g.at[jb, core, q], g.at[jb, core, q],
            ag_s.at[direction, s, q], ag_r.at[direction, s, q],
            (right, left)[direction],
        )

    def across(jb, i, q):
        return remote(
            g.at[jb, core, q], g.at[jb, core, q], d_s.at[i, q], d_r.at[i, q], partner
        )

    for q in range(2):
        total = pp[xc, q]
        for direction in range(2):
            if exists(direction, K - 1, q):
                ring(direction, K - 1, q).wait_recv()
                total = total + rrecv[direction, K - 1, q].astype(F32)
        gate, up, gh = total[:, :UB], total[:, UB : 2 * UB], total[:, 2 * UB :]
        sg = jax.nn.sigmoid(gate)
        silu = gate * sg
        g[xc, core, q, :, :UB] = (silu * up).astype(BF)
        g[xc, core, q, :, UB : 2 * UB] = (gh * up * sg * (1.0 + gate * (1.0 - sg))).astype(BF)
        g[xc, core, q, :, 2 * UB :] = (gh * silu).astype(BF)
        for direction in range(2):
            if K > 1 or q == direction:
                ag(direction, 0, q).start()
        across(xc, 0, q).start()

    def ag_exists(direction, s, q):
        return s < K - 1 or (s == K - 1 and q == direction)

    crossed = [(xc, 0, q) for q in range(2)]
    for s in range(1, K + 1):
        for q_step in range(2):
            for direction in range(2):
                q = q_step if direction == 0 else 1 - q_step
                if not ag_exists(direction, s - 1, q):
                    continue
                ag(direction, s - 1, q).wait_recv()
                if s < K and ag_exists(direction, s, q):
                    ag(direction, s, q).start()
                jb = (xc + NX - s) % NX if direction == 0 else (xc + s) % NX
                i = s if direction == 0 or s == K else NX - s
                across(jb, i, q).start()
                crossed.append((jb, i, q))
    for args in crossed:
        across(*args).wait_recv()

    acc[...] = jnp.zeros_like(acc)

    def second(jb, carry):
        at = pl.multiple_of(jb * UB, UB)
        part = g[jb].reshape(R, 3 * UB)
        acc[0] += dot(part[:, :UB], wo[0, pl.ds(at, UB), :])
        acc[1] += dot(part[:, UB : 2 * UB], wi[0, :, pl.ds(at, UB)], ((1,), (1,))) + dot(
            part[:, 2 * UB :], wi[0, :, pl.ds(pl.multiple_of(U + at, UB), UB)], ((1,), (1,))
        )
        return carry

    lax.fori_loop(0, NX, second, 0)

    bi = iota((EG * BLOCK, 1), 0)
    src, j = bi // BLOCK, bi % BLOCK
    into = iota((EG * BLOCK, QR), 1)
    pack = []
    for offset in (0, 8):
        ok = (j >= offset) & (j < offset + CAP)
        pack.append(ones_where(into == jnp.where(ok, src * CAP + j - offset, -1)))
    for i in range(4):
        block = dot(pack[0], acc[0, i * QR : (i + 1) * QR].astype(BF)) + dot(
            pack[1], acc[1, i * QR : (i + 1) * QR].astype(BF)
        )
        block = block.astype(BF)
        sa[1, i] = block[:, :HF]
        sb[1, i] = block[:, HF:]
    phase_one(1)

    rows_all = jnp.concatenate([x[h, 0].reshape(HR, F) for h in range(2)], axis=0)
    grads_all = jnp.concatenate([x[h, 1].reshape(HR, F) for h in range(2)], axis=0)

    def weight_grads(jb, carry):
        at = pl.multiple_of(jb * UB, UB)
        part = g[jb].reshape(R, 3 * UB)
        for n in range(2):
            grad_in[:, pl.ds(pl.multiple_of(n * U + at, UB), UB)] = dot(
                rows_all, part[:, (n + 1) * UB : (n + 2) * UB], ((0,), (0,))
            ).astype(BF)
        grad_out[pl.ds(at, UB), :] = dot(part[:, :UB], grads_all, ((0,), (0,))).astype(BF)
        return carry

    lax.fori_loop(0, NX // 2, weight_grads, 0)
    phase_two(1)
    lax.fori_loop(NX // 2, NX, weight_grads, 0)
    phase_end(1)

    home = jnp.concatenate(
        [r2a[1].reshape(E * BLOCK, HF), r2b[1].reshape(E * BLOCK, HF)], axis=1
    )
    mixed[...] = (wcol[0] * dot(qmat[0], home) + wcol[1] * dot(qmat[1], home)).astype(BF)
    grad_tokens[...] = dot(qmat[2], home).astype(BF)

    for copy in give_w + [give_x]:
        copy.wait_send()
    for q in range(2):
        for d in order(NZ):
            p1a(q, d).wait_send()
            p2b(q, d).wait_send()
        for d in order(NY):
            p1b(q, d).wait_send()
            p2a(q, d).wait_send()
    for direction in range(2):
        for s in range(K):
            for q in range(2):
                if exists(direction, s, q):
                    ring(direction, s, q).wait_send()
                if ag_exists(direction, s, q):
                    ag(direction, s, q).wait_send()
    for args in crossed:
        across(*args).wait_send()


def per_device(tokens, routes, route_weight, cotangent, w_in, w_out):
    T, F = tokens.shape
    E = lax.axis_size("expert")
    NX = lax.axis_size("dp") // 2
    NY = 1 << (int(math.log2(E)) // 2)
    NZ = E // NY
    U = w_out.shape[1]
    CAP = T * 2 * 5 // (4 * E)
    UB, R = U // NX, E * CAP
    HR, QR, K, HF = R // 2, R // 4, NX // 2, F // 2
    EG = E // 4
    dma = pltpu.SemaphoreType.DMA
    far = max(NZ, NY)
    vmem = pl.BlockSpec(memory_space=pltpu.VMEM)
    anywhere = pl.BlockSpec(memory_space=pl.ANY)
    mixed, grad_tokens, grad_in, grad_out = pl.pallas_call(
        functools.partial(kernel, NX, NZ, NY, CAP),
        out_shape=(
            jax.ShapeDtypeStruct((T, F), BF),
            jax.ShapeDtypeStruct((T, F), BF),
            jax.ShapeDtypeStruct((F, 2 * U), BF),
            jax.ShapeDtypeStruct((U, F), BF),
        ),
        in_specs=[vmem] * 4 + [anywhere] * 2,
        out_specs=(vmem,) * 4,
        scratch_shapes=[
            pltpu.VMEM((2, F, 2 * U), BF),
            pltpu.VMEM((2, U, F), BF),
            pltpu.VMEM((2, 4, EG * BLOCK, HF), BF),
            pltpu.VMEM((2, 4, EG * BLOCK, HF), BF),
            pltpu.VMEM((2, NZ, NY, BLOCK, HF), BF),
            pltpu.VMEM((2, NY, NZ, BLOCK, HF), BF),
            pltpu.VMEM((2, NZ, NY, BLOCK, HF), BF),
            pltpu.VMEM((2, NZ, NY, BLOCK, HF), BF),
            pltpu.VMEM((2, 2, 2, QR, F), BF),
            pltpu.VMEM((2, 2, QR, F), BF),
            pltpu.VMEM((NX, 2, QR, 3 * UB), F32),
            pltpu.VMEM((2, K, 2, QR, 3 * UB), BF),
            pltpu.VMEM((2, K, 2, QR, 3 * UB), BF),
            pltpu.VMEM((NX, 2, 2, QR, 3 * UB), BF),
            pltpu.VMEM((2, R, F), F32),
            pltpu.VMEM((3, T, E * BLOCK), BF),
            pltpu.VMEM((2, T, F), F32),
            dma((2,)), dma((2,)), dma((2,)),
            dma((2, 4, far)), dma((2, 4, far)), dma((2, 4)),
            dma, dma,
            dma((2, K, 2)), dma((2, K, 2)),
            dma((2, K, 2)), dma((2, K, 2)),
            dma((NX, 2)), dma((NX, 2)),
        ],
        compiler_params=pltpu.CompilerParams(
            collective_id=0, has_side_effects=True, vmem_limit_bytes=50 * 1024 * 1024
        ),
    )(routes.T, route_weight.T, tokens, cotangent, w_in[0], w_out[0])
    return mixed, grad_tokens, grad_in[None], grad_out[None]


def solution(mesh):
    placed = (
        P("expert", "dp"),
        P("expert", None),
        P("expert", None),
        P("expert", "dp"),
        P("expert", "dp", None),
        P("expert", None, "dp"),
    )
    return jax.shard_map(
        per_device,
        mesh=mesh,
        in_specs=placed,
        out_specs=(
            P("expert", "dp"),
            P("expert", "dp"),
            P("expert", "dp", None),
            P("expert", None, "dp"),
        ),
        check_vma=False,
    )
```

```python
import functools
import math

import jax
import jax.numpy as jnp
from jax import lax
from jax.experimental import pallas as pl
from jax.experimental.pallas import tpu as pltpu
from jax.sharding import PartitionSpec as P

BF = jnp.bfloat16
F32 = jnp.float32
MESH = pl.DeviceIdType.MESH
BLOCK = 8
HALF = 4


def dot(a, b, dims=((1,), (0,))):
    return lax.dot_general(a, b, (dims, ((), ())), preferred_element_type=F32)


def ones_where(mask):
    return jnp.where(mask, 1.0, 0.0).astype(BF)


def iota(shape, dim):
    return lax.broadcasted_iota(jnp.int32, shape, dim)


def kernel(
    NX, NZ, NY, CAP,
    routes_h, weights_h, tokens_h, cot_h, w_in, w_out,
    mixed, grad_tokens, grad_in, grad_out,
    routes, weights, tokens, cot, wi, wo, sa, sb, r1a, r1b, r2a, r2b, qmat, wcol,
    x0, xp0, pp0, rsend0, rrecv0, g0, acc0,
    x1, xp1, pp1, rsend1, rrecv1, g1, acc1,
    isem, wsend, wrecv, wlocal, asend, arecv, alocal, xsend, xrecv,
    rs_s, rs_r, ag_s, ag_r, d_s, d_r,
):
    T, F = tokens_h.shape
    U = w_out.shape[0]
    E = NZ * NY
    UB = U // NX
    K = NX // 2
    EG = E // 4
    HF = F // 2
    groups = ((0, (CAP + 1) // 2), ((CAP + 1) // 2, CAP // 2))
    x, xp, pp, rsend, rrecv = (x0, x1), (xp0, xp1), (pp0, pp1), (rsend0, rsend1), (rrecv0, rrecv1)
    g, acc = (g0, g1), (acc0, acc1)

    me_dp = lax.axis_index("dp")
    me_e = lax.axis_index("expert")
    xc, core = me_dp // 2, me_dp % 2
    Z, Y = me_e // NY, me_e % NY
    right = {"dp": ((xc + 1) % NX) * 2 + core, "expert": me_e}
    left = {"dp": ((xc + NX - 1) % NX) * 2 + core, "expert": me_e}
    partner = {"dp": xc * 2 + (1 - core), "expert": me_e}

    def z_peer(d):
        zz = (Z + d) % NZ
        return zz, {"dp": me_dp, "expert": zz * NY + Y}

    def y_peer(d):
        yy = (Y + d) % NY
        return yy, {"dp": me_dp, "expert": Z * NY + yy}

    def remote(src, dst, send, recv, device):
        return pltpu.make_async_remote_copy(
            src_ref=src, dst_ref=dst, send_sem=send, recv_sem=recv,
            device_id=device, device_id_type=MESH,
        )

    given = [
        pltpu.make_async_copy(src, dst, isem.at[i])
        for i, (src, dst) in enumerate(
            ((routes_h, routes), (weights_h, weights), (cot_h, cot), (tokens_h, tokens))
        )
    ]
    for copy in given:
        copy.start()
    barrier = pltpu.get_barrier_semaphore()
    for d in range(1, NZ):
        pl.semaphore_signal(barrier, inc=1, device_id=z_peer(d)[1], device_id_type=MESH)
    for d in range(1, NY):
        pl.semaphore_signal(barrier, inc=1, device_id=y_peer(d)[1], device_id_type=MESH)
    for device in (right, left, partner):
        pl.semaphore_signal(barrier, inc=1, device_id=device, device_id_type=MESH)

    local_w = [
        pltpu.make_async_copy(w_in, wi.at[0], wlocal.at[0]),
        pltpu.make_async_copy(w_out, wo.at[0], wlocal.at[1]),
    ]
    for copy in local_w:
        copy.start()

    upper = ones_where(iota((T, T), 0) < iota((T, T), 1))
    diagonal = iota((T, T), 0) == iota((T, T), 1)

    def slots(expert, rank, group):
        first, count = groups[group]
        inside = (rank >= first) & (rank < first + count)
        return jnp.where(inside, expert * BLOCK + rank - first, -2 * BLOCK)

    given[0].wait()
    named = [iota((E, T), 0) == routes[k : k + 1, :] for k in range(2)]
    before = dot(ones_where(named[0] | named[1]), upper)
    for copy in given[1:]:
        copy.wait()
    cot_f = cot[...].astype(F32)
    rows_of, cols_of, scaled, wcols = [], [], [], []
    for k in range(2):
        rank = jnp.sum(jnp.where(named[k], before, 0.0), axis=0, keepdims=True)
        place = routes[k : k + 1, :].astype(F32) * 16.0 + rank
        col = jnp.sum(jnp.where(diagonal, place, 0.0), axis=1, keepdims=True).astype(jnp.int32)
        wc = jnp.sum(jnp.where(diagonal, weights[k : k + 1, :], 0.0), axis=1, keepdims=True)
        rank_i = rank.astype(jnp.int32)
        rows_of.append([slots(routes[k : k + 1, :], rank_i, n) for n in range(2)])
        cols_of.append([slots(col // 16, col % 16, n) for n in range(2)])
        wcols.append(wc)
        scaled.append((wc * cot_f).astype(BF))
    token_rows = tokens[...]

    flat_sa, flat_sb = sa.reshape(2, 2, E * BLOCK, HF), sb.reshape(2, 2, E * BLOCK, HF)
    flat_ra, flat_rb = r2a.reshape(2, 2, E * BLOCK, HF), r2b.reshape(2, 2, E * BLOCK, HF)
    BR = EG * BLOCK

    def build(n):
        for i in range(2):
            ri = iota((2 * BR, T), 0) + i * 2 * BR
            a, b = rows_of[0][n], rows_of[1][n]
            block = dot(ones_where((ri == a) | (ri == b)), token_rows)
            for k in range(2):
                block += dot(ones_where(ri == rows_of[k][n] + HALF), scaled[k])
            block = block.astype(BF)
            flat_sa[0, n, 2 * i * BR : 2 * (i + 1) * BR] = block[:, :HF]
            flat_sb[0, n, 2 * i * BR : 2 * (i + 1) * BR] = block[:, HF:]

    def p1a(q, n, d):
        zz, device = z_peer(d)
        return remote(sa.at[q, n, zz], r1a.at[q, n, Z], asend.at[q, n, 0, d], arecv.at[q, n, 0, d], device)

    def p1b(q, n, d):
        yy, device = y_peer(d)
        return remote(sb.at[q, n, :, yy], r1b.at[q, n, Y], asend.at[q, n, 1, d], arecv.at[q, n, 1, d], device)

    def p2a(q, n, d):
        yy, device = y_peer(d)
        return remote(r1a.at[q, n, :, yy], r2a.at[q, n, :, Y], asend.at[q, n, 2, d], arecv.at[q, n, 2, d], device)

    def p2b(q, n, d):
        zz, device = z_peer(d)
        return remote(r1b.at[q, n, :, zz], r2b.at[q, n, Z], asend.at[q, n, 3, d], arecv.at[q, n, 3, d], device)

    def local(q, n, i):
        src, dst = (
            (sa.at[q, n, Z], r1a.at[q, n, Z]),
            (sb.at[q, n, :, Y], r1b.at[q, n, Y]),
            (r1a.at[q, n, :, Y], r2a.at[q, n, :, Y]),
            (r1b.at[q, n, :, Z], r2b.at[q, n, Z]),
        )[i]
        return pltpu.make_async_copy(src, dst, alocal.at[q, n, i])

    def order(size):
        ds = []
        for hop in range(size // 2, 0, -1):
            ds += [hop] if 2 * hop == size else [hop, size - hop]
        return ds

    def phase_one(q, n):
        for i in range(max(NZ, NY)):
            if i < len(order(NZ)):
                p1a(q, n, order(NZ)[i]).start()
            if i < len(order(NY)):
                p1b(q, n, order(NY)[i]).start()
        local(q, n, 0).start()
        local(q, n, 1).start()

    def phase_two(q, n):
        local(q, n, 0).wait()
        for d in order(NZ):
            p1a(q, n, d).wait_recv()
        for d in order(NY):
            p2a(q, n, d).start()
        local(q, n, 2).start()
        local(q, n, 1).wait()
        for d in order(NY):
            p1b(q, n, d).wait_recv()
        for d in order(NZ):
            p2b(q, n, d).start()
        local(q, n, 3).start()

    def phase_end(q, n):
        local(q, n, 2).wait()
        local(q, n, 3).wait()
        for d in order(NY):
            p2a(q, n, d).wait_recv()
        for d in order(NZ):
            p2b(q, n, d).wait_recv()

    def unpack(n):
        count = groups[n][1]
        QR = EG * count
        bj = iota((1, BR), 1)
        src, j = bj // BLOCK, bj % BLOCK
        want = iota((QR, BR), 0)
        for a in range(2):
            ok = (j >= a * HALF) & (j < a * HALF + count)
            pick = ones_where(want == jnp.where(ok, src * count + j - a * HALF, -1))
            for i in range(4):
                lo, hi = i * BR, (i + 1) * BR
                x[n][i // 2, a, i % 2, :, :HF] = dot(pick, flat_ra[0, n, lo:hi]).astype(BF)
                x[n][i // 2, a, i % 2, :, HF:] = dot(pick, flat_rb[0, n, lo:hi]).astype(BF)

    def give_x(n):
        return remote(x[n].at[1 - core], xp[n], xsend.at[n], xrecv.at[n], partner)

    def partial(n, jb):
        QR = EG * groups[n][1]
        HR = 2 * QR
        at = pl.multiple_of(jb * UB, UB)
        total, below = None, None
        for v, rows in ((0, x[n].at[core]), (1, xp[n])):
            both = jnp.concatenate(
                [wi[v, :, pl.ds(at, UB)], wi[v, :, pl.ds(pl.multiple_of(U + at, UB), UB)]], axis=1
            )
            part = dot(rows[0].reshape(HR, F), both)
            back = dot(rows[1].reshape(HR, F), wo[v, pl.ds(at, UB), :], ((1,), (1,)))
            total = part if v == 0 else total + part
            below = back if v == 0 else below + back
        for q in range(2):
            pp[n][jb, q, :, : 2 * UB] = total[q * QR : (q + 1) * QR]
            pp[n][jb, q, :, 2 * UB :] = below[q * QR : (q + 1) * QR]

    def chunk_of(direction, s):
        return (xc + K - s) % NX if direction == 0 else (xc + NX - K + s) % NX

    def ring(n, direction, s, q):
        return remote(
            rsend[n].at[direction, s, q], rrecv[n].at[direction, s, q],
            rs_s.at[n, direction, s, q], rs_r.at[n, direction, s, q],
            (right, left)[direction],
        )

    def exists(direction, s, q):
        return s > 0 or q == direction

    def ring_step(n, direction, s, q):
        value = pp[n][chunk_of(direction, s), q]
        if s > 0 and exists(direction, s - 1, q):
            ring(n, direction, s - 1, q).wait_recv()
            value = value + rrecv[n][direction, s - 1, q].astype(F32)
        rsend[n][direction, s, q] = value.astype(BF)
        ring(n, direction, s, q).start()

    def ring_first(n):
        partial(n, (xc + K) % NX)
        for direction in range(2):
            ring_step(n, direction, 0, direction)
        if K > 1:
            for direction in range(2):
                partial(n, chunk_of(direction, 1))
                ring_step(n, direction, 1, 1 - direction)
        else:
            partial(n, xc)

    def ring_ahead(n, s):
        if s < K:
            for direction in range(2):
                partial(n, chunk_of(direction, s))
        elif s == K:
            partial(n, xc)

    def ring_round(n, s):
        if s >= K:
            return
        for far in (1, 0):
            for direction in range(2):
                if not (s == 1 and far == 1):
                    ring_step(n, direction, s, far if direction == 0 else 1 - far)
        ring_ahead(n, s + 1)

    def ag(n, direction, s, q):
        jb = (xc + NX - s) % NX if direction == 0 else (xc + s) % NX
        return remote(
            g[n].at[jb, core, q], g[n].at[jb, core, q],
            ag_s.at[n, direction, s, q], ag_r.at[n, direction, s, q],
            (right, left)[direction],
        )

    def across(n, jb, i, q):
        return remote(
            g[n].at[jb, core, q], g[n].at[jb, core, q], d_s.at[n, i, q], d_r.at[n, i, q], partner
        )

    def ag_exists(direction, s, q):
        return s < K - 1 or (s == K - 1 and q == direction)

    crossed = ([], [])

    def activate(n):
        for q in range(2):
            total = pp[n][xc, q]
            for direction in range(2):
                if exists(direction, K - 1, q):
                    ring(n, direction, K - 1, q).wait_recv()
                    total = total + rrecv[n][direction, K - 1, q].astype(F32)
            gate, up, gh = total[:, :UB], total[:, UB : 2 * UB], total[:, 2 * UB :]
            sg = jax.nn.sigmoid(gate)
            silu = gate * sg
            g[n][xc, core, q, :, :UB] = (silu * up).astype(BF)
            g[n][xc, core, q, :, UB : 2 * UB] = (gh * up * sg * (1.0 + gate * (1.0 - sg))).astype(BF)
            g[n][xc, core, q, :, 2 * UB :] = (gh * silu).astype(BF)
            for direction in range(2):
                if ag_exists(direction, 0, q):
                    ag(n, direction, 0, q).start()
            across(n, xc, 0, q).start()
            crossed[n].append((n, xc, 0, q))

    def gather_round(n, s):
        if s > K:
            return
        for q_step in range(2):
            for direction in range(2):
                q = q_step if direction == 0 else 1 - q_step
                if not ag_exists(direction, s - 1, q):
                    continue
                ag(n, direction, s - 1, q).wait_recv()
                if s < K and ag_exists(direction, s, q):
                    ag(n, direction, s, q).start()
                jb = (xc + NX - s) % NX if direction == 0 else (xc + s) % NX
                i = s if direction == 0 or s == K else NX - s
                across(n, jb, i, q).start()
                crossed[n].append((n, jb, i, q))

    def second(n, s):
        R = E * groups[n][1]
        todo = [args for args in crossed[n] if args[2] == s or args[2] == NX - s]
        for args in todo:
            across(*args).wait_recv()
        for jb in [args[1] for args in todo if args[3] == 0]:
            at = pl.multiple_of(jb * UB, UB)
            part = g[n][jb].reshape(R, 3 * UB)
            both = jnp.concatenate(
                [wi[0, :, pl.ds(at, UB)], wi[0, :, pl.ds(pl.multiple_of(U + at, UB), UB)]], axis=1
            )
            down = dot(part[:, :UB], wo[0, pl.ds(at, UB), :])
            back = dot(part[:, UB:], both, ((1,), (1,)))
            if s == 0:
                acc[n][0] = down
                acc[n][1] = back
            else:
                acc[n][0] += down
                acc[n][1] += back

    def pack(n):
        count = groups[n][1]
        QR = EG * count
        bi = iota((BR, 1), 0)
        src, j = bi // BLOCK, bi % BLOCK
        into = iota((BR, QR), 1)
        puts = []
        for a in range(2):
            ok = (j >= a * HALF) & (j < a * HALF + count)
            puts.append(ones_where(into == jnp.where(ok, src * count + j - a * HALF, -1)))
        for i in range(4):
            rows = slice(i * QR, (i + 1) * QR)
            block = dot(puts[0], acc[n][0, rows].astype(BF)) + dot(puts[1], acc[n][1, rows].astype(BF))
            block = block.astype(BF)
            flat_sa[1, n, i * BR : (i + 1) * BR] = block[:, :HF]
            flat_sb[1, n, i * BR : (i + 1) * BR] = block[:, HF:]

    def way_back(n):
        second(n, K)
        pack(n)
        phase_one(1, n)

    def weight_grads(jb, carry):
        at = pl.multiple_of(jb * UB, UB)
        ups, downs = [None, None], None
        for n in range(2):
            R = E * groups[n][1]
            part = g[n][jb].reshape(R, 3 * UB)
            rows = jnp.concatenate([x[n][h, 0].reshape(R // 2, F) for h in range(2)], axis=0)
            grads = jnp.concatenate([x[n][h, 1].reshape(R // 2, F) for h in range(2)], axis=0)
            for m in range(2):
                term = dot(rows, part[:, (m + 1) * UB : (m + 2) * UB], ((0,), (0,)))
                ups[m] = term if n == 0 else ups[m] + term
            term = dot(part[:, :UB], grads, ((0,), (0,)))
            downs = term if n == 0 else downs + term
        for m in range(2):
            grad_in[:, pl.ds(pl.multiple_of(m * U + at, UB), UB)] = ups[m].astype(BF)
        grad_out[pl.ds(at, UB), :] = downs.astype(BF)
        return carry

    build(0)
    pl.semaphore_wait(barrier, NZ + NY + 1)
    phase_one(0, 0)
    give_w = [
        remote(w_in, wi.at[1], wsend.at[0], wrecv.at[0], partner),
        remote(w_out, wo.at[1], wsend.at[1], wrecv.at[1], partner),
    ]
    for copy in give_w:
        copy.start()
    build(1)
    phase_two(0, 0)
    phase_one(0, 1)
    for k in range(2):
        wcol[k] = jnp.broadcast_to(wcols[k], (T, F))
    ci = iota((T, E * BLOCK), 1)
    for n in range(2):
        for k in range(2):
            qmat[n, k] = ones_where(ci == cols_of[k][n])
        qmat[n, 2] = ones_where((ci == cols_of[0][n] + HALF) | (ci == cols_of[1][n] + HALF))
    phase_end(0, 0)
    unpack(0)
    give_x(0).start()
    phase_two(0, 1)
    for copy in local_w:
        copy.wait()
    for copy in give_w:
        copy.wait_recv()
    give_x(0).wait_recv()
    ring_first(0)

    def start_second_group():
        phase_end(0, 1)
        unpack(1)
        give_x(1).start()
        give_x(1).wait_recv()
        ring_first(1)

    def gather_and_use(n, s):
        gather_round(n, s)
        second(n, s - 1)

    def events(n):
        rounds = [functools.partial(ring_round, n, s) for s in range(1, K)]
        rounds.append(functools.partial(activate, n))
        return rounds + [functools.partial(gather_and_use, n, s) for s in range(1, K + 1)]

    lead = 2
    first_events, second_events = events(0), [start_second_group] + events(1)
    for i in range(lead + len(second_events)):
        if i < len(first_events):
            first_events[i]()
        if i == len(first_events):
            way_back(0)
        if i >= lead:
            second_events[i - lead]()
    way_back(1)
    phase_two(1, 0)
    lax.fori_loop(0, NX // 2, weight_grads, 0)
    phase_two(1, 1)
    lax.fori_loop(NX // 2, NX, weight_grads, 0)

    sums = [None] * 3
    for n in range(2):
        phase_end(1, n)
        home = jnp.concatenate([flat_ra[1, n], flat_rb[1, n]], axis=1)
        for k in range(3):
            term = dot(qmat[n, k], home)
            sums[k] = term if n == 0 else sums[k] + term
    mixed[...] = (wcol[0] * sums[0] + wcol[1] * sums[1]).astype(BF)
    grad_tokens[...] = sums[2].astype(BF)

    for copy in give_w:
        copy.wait_send()
    for n in range(2):
        give_x(n).wait_send()
        for q in range(2):
            for d in order(NZ):
                p1a(q, n, d).wait_send()
                p2b(q, n, d).wait_send()
            for d in order(NY):
                p1b(q, n, d).wait_send()
                p2a(q, n, d).wait_send()
        for direction in range(2):
            for s in range(K):
                for q in range(2):
                    if exists(direction, s, q):
                        ring(n, direction, s, q).wait_send()
                    if ag_exists(direction, s, q):
                        ag(n, direction, s, q).wait_send()
        for args in crossed[n]:
            across(*args).wait_send()


def put_out(a, b, c, d, a_out, b_out, c_out, d_out, sem):
    pairs = ((c, c_out), (d, d_out), (a, a_out), (b, b_out))
    copies = [pltpu.make_async_copy(src, dst, sem.at[i]) for i, (src, dst) in enumerate(pairs)]
    for copy in copies:
        copy.start()
    for copy in copies:
        copy.wait()


def per_device(tokens, routes, route_weight, cotangent, w_in, w_out):
    T, F = tokens.shape
    E = lax.axis_size("expert")
    NX = lax.axis_size("dp") // 2
    NY = 1 << (int(math.log2(E)) // 2)
    NZ = E // NY
    U = w_out.shape[1]
    CAP = T * 2 * 5 // (4 * E)
    UB, K, HF, EG = U // NX, NX // 2, F // 2, E // 4
    dma = pltpu.SemaphoreType.DMA
    far = max(NZ, NY)
    vmem = pl.BlockSpec(memory_space=pltpu.VMEM)
    anywhere = pl.BlockSpec(memory_space=pl.ANY)

    def of_group(count):
        QR = EG * count
        return (
            pltpu.VMEM((2, 2, 2, QR, F), BF),
            pltpu.VMEM((2, 2, QR, F), BF),
            pltpu.VMEM((NX, 2, QR, 3 * UB), F32),
            pltpu.VMEM((2, K, 2, QR, 3 * UB), BF),
            pltpu.VMEM((2, K, 2, QR, 3 * UB), BF),
            pltpu.VMEM((NX, 2, 2, QR, 3 * UB), BF),
            pltpu.VMEM((2, 4 * QR, F), F32),
        )

    results = pl.pallas_call(
        functools.partial(kernel, NX, NZ, NY, CAP),
        out_shape=(
            jax.ShapeDtypeStruct((T, F), BF),
            jax.ShapeDtypeStruct((T, F), BF),
            jax.ShapeDtypeStruct((F, 2 * U), BF),
            jax.ShapeDtypeStruct((U, F), BF),
        ),
        in_specs=[pl.BlockSpec(memory_space=pltpu.HBM)] * 6,
        out_specs=(vmem,) * 4,
        scratch_shapes=[
            pltpu.VMEM((2, T), jnp.int32),
            pltpu.VMEM((2, T), F32),
            pltpu.VMEM((T, F), BF),
            pltpu.VMEM((T, F), BF),
            pltpu.VMEM((2, F, 2 * U), BF),
            pltpu.VMEM((2, U, F), BF),
            pltpu.VMEM((2, 2, NZ, NY, BLOCK, HF), BF),
            pltpu.VMEM((2, 2, NZ, NY, BLOCK, HF), BF),
            pltpu.VMEM((2, 2, NZ, NY, BLOCK, HF), BF),
            pltpu.VMEM((2, 2, NY, NZ, BLOCK, HF), BF),
            pltpu.VMEM((2, 2, NZ, NY, BLOCK, HF), BF),
            pltpu.VMEM((2, 2, NZ, NY, BLOCK, HF), BF),
            pltpu.VMEM((2, 3, T, E * BLOCK), BF),
            pltpu.VMEM((2, T, F), F32),
            *of_group((CAP + 1) // 2),
            *of_group(CAP // 2),
            dma((4,)), dma((2,)), dma((2,)), dma((2,)),
            dma((2, 2, 4, far)), dma((2, 2, 4, far)), dma((2, 2, 4)),
            dma((2,)), dma((2,)),
            dma((2, 2, K, 2)), dma((2, 2, K, 2)),
            dma((2, 2, K, 2)), dma((2, 2, K, 2)),
            dma((2, NX, 2)), dma((2, NX, 2)),
        ],
        compiler_params=pltpu.CompilerParams(
            collective_id=0, has_side_effects=True, vmem_limit_bytes=50 * 1024 * 1024
        ),
    )(
        *(
            pltpu.with_memory_space_constraint(v, pltpu.HBM)
            for v in (routes.T, route_weight.T, tokens, cotangent, w_in[0], w_out[0])
        )
    )
    mixed, grad_tokens, grad_in, grad_out = pl.pallas_call(
        put_out,
        out_shape=tuple(jax.ShapeDtypeStruct(r.shape, r.dtype) for r in results),
        in_specs=[anywhere] * 4,
        out_specs=(pl.BlockSpec(memory_space=pltpu.HBM),) * 4,
        scratch_shapes=[dma((4,))],
        compiler_params=pltpu.CompilerParams(vmem_limit_bytes=1024 * 1024),
    )(*results)
    return mixed, grad_tokens, grad_in[None], grad_out[None]


def solution(mesh):
    placed = (
        P("expert", "dp"),
        P("expert", None),
        P("expert", None),
        P("expert", "dp"),
        P("expert", "dp", None),
        P("expert", None, "dp"),
    )
    return jax.shard_map(
        per_device,
        mesh=mesh,
        in_specs=placed,
        out_specs=(
            P("expert", "dp"),
            P("expert", "dp"),
            P("expert", "dp", None),
            P("expert", None, "dp"),
        ),
        check_vma=False,
    )
```

```python
import functools
import math

import jax
import jax.numpy as jnp
from jax import lax
from jax.experimental import pallas as pl
from jax.experimental.pallas import tpu as pltpu
from jax.sharding import PartitionSpec as P

BF = jnp.bfloat16
F32 = jnp.float32
MESH = pl.DeviceIdType.MESH
BLOCK = 8
HALF = 4


def dot(a, b, dims=((1,), (0,))):
    return lax.dot_general(a, b, (dims, ((), ())), preferred_element_type=F32)


def ones_where(mask):
    return jnp.where(mask, 1.0, 0.0).astype(BF)


def iota(shape, dim):
    return lax.broadcasted_iota(jnp.int32, shape, dim)


def kernel(
    NX, NZ, NY, CAP,
    routes_h, weights_h, tokens_h, cot_h, w_in, w_out,
    mixed, grad_tokens, grad_in, grad_out,
    routes, weights, tokens, cot, wi, wo, sa, sb, r1a, r1b, r2a, r2b, qmat, wcol,
    x0, xp0, pp0, rsend0, rrecv0, g0, acc0,
    x1, xp1, pp1, rsend1, rrecv1, g1, acc1,
    isem, wsend, wrecv, wlocal, asend, arecv, alocal, xsend, xrecv,
    rs_s, rs_r, ag_s, ag_r, d_s, d_r,
):
    T, F = tokens_h.shape
    U = w_out.shape[0]
    E = NZ * NY
    UB = U // NX
    K = NX // 2
    EG = E // 4
    HF = F // 2
    groups = ((0, (CAP + 1) // 2), ((CAP + 1) // 2, CAP // 2))
    x, xp, pp, rsend, rrecv = (x0, x1), (xp0, xp1), (pp0, pp1), (rsend0, rsend1), (rrecv0, rrecv1)
    g, acc = (g0, g1), (acc0, acc1)

    me_dp = lax.axis_index("dp")
    me_e = lax.axis_index("expert")
    xc, core = me_dp // 2, me_dp % 2
    Z, Y = me_e // NY, me_e % NY
    right = {"dp": ((xc + 1) % NX) * 2 + core, "expert": me_e}
    left = {"dp": ((xc + NX - 1) % NX) * 2 + core, "expert": me_e}
    partner = {"dp": xc * 2 + (1 - core), "expert": me_e}

    def z_peer(d):
        zz = (Z + d) % NZ
        return zz, {"dp": me_dp, "expert": zz * NY + Y}

    def y_peer(d):
        yy = (Y + d) % NY
        return yy, {"dp": me_dp, "expert": Z * NY + yy}

    def remote(src, dst, send, recv, device):
        return pltpu.make_async_remote_copy(
            src_ref=src, dst_ref=dst, send_sem=send, recv_sem=recv,
            device_id=device, device_id_type=MESH,
        )

    given = [
        pltpu.make_async_copy(src, dst, isem.at[i])
        for i, (src, dst) in enumerate(
            ((routes_h, routes), (weights_h, weights), (cot_h, cot), (tokens_h, tokens))
        )
    ]
    for copy in given:
        copy.start()
    barrier = pltpu.get_barrier_semaphore()
    for d in range(1, NZ):
        pl.semaphore_signal(barrier, inc=1, device_id=z_peer(d)[1], device_id_type=MESH)
    for d in range(1, NY):
        pl.semaphore_signal(barrier, inc=1, device_id=y_peer(d)[1], device_id_type=MESH)
    for device in (right, left, partner):
        pl.semaphore_signal(barrier, inc=1, device_id=device, device_id_type=MESH)

    local_w = [
        pltpu.make_async_copy(w_in, wi.at[0], wlocal.at[0]),
        pltpu.make_async_copy(w_out, wo.at[0], wlocal.at[1]),
    ]
    for copy in local_w:
        copy.start()

    upper = ones_where(iota((T, T), 0) < iota((T, T), 1))
    diagonal = iota((T, T), 0) == iota((T, T), 1)

    def slots(expert, rank, group):
        first, count = groups[group]
        inside = (rank >= first) & (rank < first + count)
        return jnp.where(inside, expert * BLOCK + rank - first, -2 * BLOCK)

    given[0].wait()
    named = [iota((E, T), 0) == routes[k : k + 1, :] for k in range(2)]
    before = dot(ones_where(named[0] | named[1]), upper)
    for copy in given[1:]:
        copy.wait()
    cot_f = cot[...].astype(F32)
    rows_of, cols_of, scaled, wcols = [], [], [], []
    for k in range(2):
        rank = jnp.sum(jnp.where(named[k], before, 0.0), axis=0, keepdims=True)
        place = routes[k : k + 1, :].astype(F32) * 16.0 + rank
        col = jnp.sum(jnp.where(diagonal, place, 0.0), axis=1, keepdims=True).astype(jnp.int32)
        wc = jnp.sum(jnp.where(diagonal, weights[k : k + 1, :], 0.0), axis=1, keepdims=True)
        rank_i = rank.astype(jnp.int32)
        rows_of.append([slots(routes[k : k + 1, :], rank_i, n) for n in range(2)])
        cols_of.append([slots(col // 16, col % 16, n) for n in range(2)])
        wcols.append(wc)
        scaled.append((wc * cot_f).astype(BF))
    token_rows = tokens[...]

    flat_sa, flat_sb = sa.reshape(2, 2, E * BLOCK, HF), sb.reshape(2, 2, E * BLOCK, HF)
    flat_ra, flat_rb = r2a.reshape(2, 2, E * BLOCK, HF), r2b.reshape(2, 2, E * BLOCK, HF)
    BR = EG * BLOCK

    def build(n):
        for i in range(2):
            ri = iota((2 * BR, T), 0) + i * 2 * BR
            a, b = rows_of[0][n], rows_of[1][n]
            block = dot(ones_where((ri == a) | (ri == b)), token_rows)
            for k in range(2):
                block += dot(ones_where(ri == rows_of[k][n] + HALF), scaled[k])
            block = block.astype(BF)
            flat_sa[0, n, 2 * i * BR : 2 * (i + 1) * BR] = block[:, :HF]
            flat_sb[0, n, 2 * i * BR : 2 * (i + 1) * BR] = block[:, HF:]

    def p1a(q, n, d):
        zz, device = z_peer(d)
        return remote(sa.at[q, n, zz], r1a.at[q, n, Z], asend.at[q, n, 0, d], arecv.at[q, n, 0, d], device)

    def p1b(q, n, d):
        yy, device = y_peer(d)
        return remote(sb.at[q, n, :, yy], r1b.at[q, n, Y], asend.at[q, n, 1, d], arecv.at[q, n, 1, d], device)

    def p2a(q, n, d):
        yy, device = y_peer(d)
        return remote(r1a.at[q, n, :, yy], r2a.at[q, n, :, Y], asend.at[q, n, 2, d], arecv.at[q, n, 2, d], device)

    def p2b(q, n, d):
        zz, device = z_peer(d)
        return remote(r1b.at[q, n, :, zz], r2b.at[q, n, Z], asend.at[q, n, 3, d], arecv.at[q, n, 3, d], device)

    def local(q, n, i):
        src, dst = (
            (sa.at[q, n, Z], r1a.at[q, n, Z]),
            (sb.at[q, n, :, Y], r1b.at[q, n, Y]),
            (r1a.at[q, n, :, Y], r2a.at[q, n, :, Y]),
            (r1b.at[q, n, :, Z], r2b.at[q, n, Z]),
        )[i]
        return pltpu.make_async_copy(src, dst, alocal.at[q, n, i])

    def order(size):
        ds = []
        for hop in range(size // 2, 0, -1):
            ds += [hop] if 2 * hop == size else [hop, size - hop]
        return ds

    def phase_one(q, n):
        for i in range(max(NZ, NY)):
            if i < len(order(NZ)):
                p1a(q, n, order(NZ)[i]).start()
            if i < len(order(NY)):
                p1b(q, n, order(NY)[i]).start()
        local(q, n, 0).start()
        local(q, n, 1).start()

    def phase_two(q, n):
        local(q, n, 0).wait()
        for d in order(NZ):
            p1a(q, n, d).wait_recv()
        for d in order(NY):
            p2a(q, n, d).start()
        local(q, n, 2).start()
        local(q, n, 1).wait()
        for d in order(NY):
            p1b(q, n, d).wait_recv()
        for d in order(NZ):
            p2b(q, n, d).start()
        local(q, n, 3).start()

    def phase_end(q, n):
        local(q, n, 2).wait()
        local(q, n, 3).wait()
        for d in order(NY):
            p2a(q, n, d).wait_recv()
        for d in order(NZ):
            p2b(q, n, d).wait_recv()

    def unpack(n):
        count = groups[n][1]
        QR = EG * count
        bj = iota((1, BR), 1)
        src, j = bj // BLOCK, bj % BLOCK
        want = iota((QR, BR), 0)
        for a in range(2):
            ok = (j >= a * HALF) & (j < a * HALF + count)
            pick = ones_where(want == jnp.where(ok, src * count + j - a * HALF, -1))
            for i in range(4):
                lo, hi = i * BR, (i + 1) * BR
                x[n][i // 2, a, i % 2, :, :HF] = dot(pick, flat_ra[0, n, lo:hi]).astype(BF)
                x[n][i // 2, a, i % 2, :, HF:] = dot(pick, flat_rb[0, n, lo:hi]).astype(BF)

    def give_x(n):
        return remote(x[n].at[1 - core], xp[n], xsend.at[n], xrecv.at[n], partner)

    def partial(n, jb):
        QR = EG * groups[n][1]
        HR = 2 * QR
        at = pl.multiple_of(jb * UB, UB)
        total, below = None, None
        for v, rows in ((0, x[n].at[core]), (1, xp[n])):
            both = jnp.concatenate(
                [wi[v, :, pl.ds(at, UB)], wi[v, :, pl.ds(pl.multiple_of(U + at, UB), UB)]], axis=1
            )
            part = dot(rows[0].reshape(HR, F), both)
            back = dot(rows[1].reshape(HR, F), wo[v, pl.ds(at, UB), :], ((1,), (1,)))
            total = part if v == 0 else total + part
            below = back if v == 0 else below + back
        for q in range(2):
            pp[n][jb, q, :, : 2 * UB] = total[q * QR : (q + 1) * QR]
            pp[n][jb, q, :, 2 * UB :] = below[q * QR : (q + 1) * QR]

    def chunk_of(direction, s):
        return (xc + K - s) % NX if direction == 0 else (xc + NX - K + s) % NX

    def ring(n, direction, s, q):
        return remote(
            rsend[n].at[direction, s, q], rrecv[n].at[direction, s, q],
            rs_s.at[n, direction, s, q], rs_r.at[n, direction, s, q],
            (right, left)[direction],
        )

    def exists(direction, s, q):
        return s > 0 or q == direction

    def ring_step(n, direction, s, q):
        value = pp[n][chunk_of(direction, s), q]
        if s > 0 and exists(direction, s - 1, q):
            ring(n, direction, s - 1, q).wait_recv()
            value = value + rrecv[n][direction, s - 1, q].astype(F32)
        rsend[n][direction, s, q] = value.astype(BF)
        ring(n, direction, s, q).start()

    def ring_first(n):
        partial(n, (xc + K) % NX)
        for direction in range(2):
            ring_step(n, direction, 0, direction)
        if K > 1:
            for direction in range(2):
                partial(n, chunk_of(direction, 1))
                ring_step(n, direction, 1, 1 - direction)
        else:
            partial(n, xc)

    def ring_ahead(n, s):
        if s < K:
            for direction in range(2):
                partial(n, chunk_of(direction, s))
        elif s == K:
            partial(n, xc)

    def ring_round(n, s):
        if s >= K:
            return
        for far in (1, 0):
            for direction in range(2):
                if not (s == 1 and far == 1):
                    ring_step(n, direction, s, far if direction == 0 else 1 - far)
        ring_ahead(n, s + 1)

    def ag(n, direction, s, q):
        jb = (xc + NX - s) % NX if direction == 0 else (xc + s) % NX
        return remote(
            g[n].at[jb, core, q], g[n].at[jb, core, q],
            ag_s.at[n, direction, s, q], ag_r.at[n, direction, s, q],
            (right, left)[direction],
        )

    def across(n, jb, i, q):
        return remote(
            g[n].at[jb, core, q], g[n].at[jb, core, q], d_s.at[n, i, q], d_r.at[n, i, q], partner
        )

    def ag_exists(direction, s, q):
        return s < K - 1 or (s == K - 1 and q == direction)

    crossed = ([], [])

    def activate(n):
        for q in range(2):
            total = pp[n][xc, q]
            for direction in range(2):
                if exists(direction, K - 1, q):
                    ring(n, direction, K - 1, q).wait_recv()
                    total = total + rrecv[n][direction, K - 1, q].astype(F32)
            gate, up, gh = total[:, :UB], total[:, UB : 2 * UB], total[:, 2 * UB :]
            sg = jax.nn.sigmoid(gate)
            silu = gate * sg
            g[n][xc, core, q, :, :UB] = (silu * up).astype(BF)
            g[n][xc, core, q, :, UB : 2 * UB] = (gh * up * sg * (1.0 + gate * (1.0 - sg))).astype(BF)
            g[n][xc, core, q, :, 2 * UB :] = (gh * silu).astype(BF)
            for direction in range(2):
                if ag_exists(direction, 0, q):
                    ag(n, direction, 0, q).start()
            across(n, xc, 0, q).start()
            crossed[n].append((n, xc, 0, q))

    def gather_round(n, s):
        if s > K:
            return
        for q_step in range(2):
            for direction in range(2):
                q = q_step if direction == 0 else 1 - q_step
                if not ag_exists(direction, s - 1, q):
                    continue
                ag(n, direction, s - 1, q).wait_recv()
                if s < K and ag_exists(direction, s, q):
                    ag(n, direction, s, q).start()
                jb = (xc + NX - s) % NX if direction == 0 else (xc + s) % NX
                i = s if direction == 0 or s == K else NX - s
                across(n, jb, i, q).start()
                crossed[n].append((n, jb, i, q))

    def second(n, s):
        R = E * groups[n][1]
        todo = [args for args in crossed[n] if args[2] == s or args[2] == NX - s]
        for args in todo:
            across(*args).wait_recv()
        for jb in [args[1] for args in todo if args[3] == 0]:
            at = pl.multiple_of(jb * UB, UB)
            part = g[n][jb].reshape(R, 3 * UB)
            both = jnp.concatenate(
                [wi[0, :, pl.ds(at, UB)], wi[0, :, pl.ds(pl.multiple_of(U + at, UB), UB)]], axis=1
            )
            down = dot(part[:, :UB], wo[0, pl.ds(at, UB), :])
            back = dot(part[:, UB:], both, ((1,), (1,)))
            if s == 0:
                acc[n][0] = down
                acc[n][1] = back
            else:
                acc[n][0] += down
                acc[n][1] += back

    def pack(n):
        count = groups[n][1]
        QR = EG * count
        bi = iota((BR, 1), 0)
        src, j = bi // BLOCK, bi % BLOCK
        into = iota((BR, QR), 1)
        puts = []
        for a in range(2):
            ok = (j >= a * HALF) & (j < a * HALF + count)
            puts.append(ones_where(into == jnp.where(ok, src * count + j - a * HALF, -1)))
        for i in range(4):
            rows = slice(i * QR, (i + 1) * QR)
            block = dot(puts[0], acc[n][0, rows].astype(BF)) + dot(puts[1], acc[n][1, rows].astype(BF))
            block = block.astype(BF)
            flat_sa[1, n, i * BR : (i + 1) * BR] = block[:, :HF]
            flat_sb[1, n, i * BR : (i + 1) * BR] = block[:, HF:]

    def way_back(n):
        second(n, K)
        pack(n)
        phase_one(1, n)

    def weight_grads(jb, carry):
        at = pl.multiple_of(jb * UB, UB)
        ups, downs = [None, None], None
        for n in range(2):
            R = E * groups[n][1]
            part = g[n][jb].reshape(R, 3 * UB)
            rows = jnp.concatenate([x[n][h, 0].reshape(R // 2, F) for h in range(2)], axis=0)
            grads = jnp.concatenate([x[n][h, 1].reshape(R // 2, F) for h in range(2)], axis=0)
            for m in range(2):
                term = dot(rows, part[:, (m + 1) * UB : (m + 2) * UB], ((0,), (0,)))
                ups[m] = term if n == 0 else ups[m] + term
            term = dot(part[:, :UB], grads, ((0,), (0,)))
            downs = term if n == 0 else downs + term
        for m in range(2):
            grad_in[:, pl.ds(pl.multiple_of(m * U + at, UB), UB)] = ups[m].astype(BF)
        grad_out[pl.ds(at, UB), :] = downs.astype(BF)
        return carry

    build(0)
    pl.semaphore_wait(barrier, NZ + NY + 1)
    phase_one(0, 0)
    build(1)
    phase_one(0, 1)
    give_w = [
        remote(w_in, wi.at[1], wsend.at[0], wrecv.at[0], partner),
        remote(w_out, wo.at[1], wsend.at[1], wrecv.at[1], partner),
    ]
    for copy in give_w:
        copy.start()
    for k in range(2):
        wcol[k] = jnp.broadcast_to(wcols[k], (T, F))
    phase_two(0, 0)
    ci = iota((T, E * BLOCK), 1)
    for n in range(2):
        for k in range(2):
            qmat[n, k] = ones_where(ci == cols_of[k][n])
        qmat[n, 2] = ones_where((ci == cols_of[0][n] + HALF) | (ci == cols_of[1][n] + HALF))
    phase_two(0, 1)
    phase_end(0, 0)
    unpack(0)
    give_x(0).start()
    for copy in local_w:
        copy.wait()
    for copy in give_w:
        copy.wait_recv()
    give_x(0).wait_recv()
    ring_first(0)
    phase_end(0, 1)
    unpack(1)
    give_x(1).start()
    ring_round(0, 1)
    give_x(1).wait_recv()
    ring_first(1)
    for s in range(2, K):
        ring_round(0, s)
        ring_round(1, s - 1)
    activate(0)
    if K > 1:
        ring_round(1, K - 1)
    gather_round(0, 1)
    activate(1)
    second(0, 0)
    for s in range(2, K):
        gather_round(0, s)
        second(0, s - 1)
        gather_round(1, s - 1)
        second(1, s - 2)
    if K > 1:
        gather_round(0, K)
        second(0, K - 1)
        gather_round(1, K - 1)
        second(1, K - 2)
    way_back(0)
    gather_round(1, K)
    second(1, K - 1)
    way_back(1)
    phase_two(1, 0)
    lax.fori_loop(0, NX // 2, weight_grads, 0)
    phase_two(1, 1)
    lax.fori_loop(NX // 2, NX, weight_grads, 0)

    sums = [None] * 3
    for n in range(2):
        phase_end(1, n)
        home = jnp.concatenate([flat_ra[1, n], flat_rb[1, n]], axis=1)
        for k in range(3):
            term = dot(qmat[n, k], home)
            sums[k] = term if n == 0 else sums[k] + term
    mixed[...] = (wcol[0] * sums[0] + wcol[1] * sums[1]).astype(BF)
    grad_tokens[...] = sums[2].astype(BF)

    for copy in give_w:
        copy.wait_send()
    for n in range(2):
        give_x(n).wait_send()
        for q in range(2):
            for d in order(NZ):
                p1a(q, n, d).wait_send()
                p2b(q, n, d).wait_send()
            for d in order(NY):
                p1b(q, n, d).wait_send()
                p2a(q, n, d).wait_send()
        for direction in range(2):
            for s in range(K):
                for q in range(2):
                    if exists(direction, s, q):
                        ring(n, direction, s, q).wait_send()
                    if ag_exists(direction, s, q):
                        ag(n, direction, s, q).wait_send()
        for args in crossed[n]:
            across(*args).wait_send()


def put_out(a, b, c, d, a_out, b_out, c_out, d_out, sem):
    pairs = ((c, c_out), (d, d_out), (a, a_out), (b, b_out))
    copies = [pltpu.make_async_copy(src, dst, sem.at[i]) for i, (src, dst) in enumerate(pairs)]
    for copy in copies:
        copy.start()
    for copy in copies:
        copy.wait()


def per_device(tokens, routes, route_weight, cotangent, w_in, w_out):
    T, F = tokens.shape
    E = lax.axis_size("expert")
    NX = lax.axis_size("dp") // 2
    NY = 1 << (int(math.log2(E)) // 2)
    NZ = E // NY
    U = w_out.shape[1]
    CAP = T * 2 * 5 // (4 * E)
    UB, K, HF, EG = U // NX, NX // 2, F // 2, E // 4
    dma = pltpu.SemaphoreType.DMA
    far = max(NZ, NY)
    vmem = pl.BlockSpec(memory_space=pltpu.VMEM)
    anywhere = pl.BlockSpec(memory_space=pl.ANY)

    def of_group(count):
        QR = EG * count
        return (
            pltpu.VMEM((2, 2, 2, QR, F), BF),
            pltpu.VMEM((2, 2, QR, F), BF),
            pltpu.VMEM((NX, 2, QR, 3 * UB), F32),
            pltpu.VMEM((2, K, 2, QR, 3 * UB), BF),
            pltpu.VMEM((2, K, 2, QR, 3 * UB), BF),
            pltpu.VMEM((NX, 2, 2, QR, 3 * UB), BF),
            pltpu.VMEM((2, 4 * QR, F), F32),
        )

    results = pl.pallas_call(
        functools.partial(kernel, NX, NZ, NY, CAP),
        out_shape=(
            jax.ShapeDtypeStruct((T, F), BF),
            jax.ShapeDtypeStruct((T, F), BF),
            jax.ShapeDtypeStruct((F, 2 * U), BF),
            jax.ShapeDtypeStruct((U, F), BF),
        ),
        in_specs=[pl.BlockSpec(memory_space=pltpu.HBM)] * 6,
        out_specs=(vmem,) * 4,
        scratch_shapes=[
            pltpu.VMEM((2, T), jnp.int32),
            pltpu.VMEM((2, T), F32),
            pltpu.VMEM((T, F), BF),
            pltpu.VMEM((T, F), BF),
            pltpu.VMEM((2, F, 2 * U), BF),
            pltpu.VMEM((2, U, F), BF),
            pltpu.VMEM((2, 2, NZ, NY, BLOCK, HF), BF),
            pltpu.VMEM((2, 2, NZ, NY, BLOCK, HF), BF),
            pltpu.VMEM((2, 2, NZ, NY, BLOCK, HF), BF),
            pltpu.VMEM((2, 2, NY, NZ, BLOCK, HF), BF),
            pltpu.VMEM((2, 2, NZ, NY, BLOCK, HF), BF),
            pltpu.VMEM((2, 2, NZ, NY, BLOCK, HF), BF),
            pltpu.VMEM((2, 3, T, E * BLOCK), BF),
            pltpu.VMEM((2, T, F), F32),
            *of_group((CAP + 1) // 2),
            *of_group(CAP // 2),
            dma((4,)), dma((2,)), dma((2,)), dma((2,)),
            dma((2, 2, 4, far)), dma((2, 2, 4, far)), dma((2, 2, 4)),
            dma((2,)), dma((2,)),
            dma((2, 2, K, 2)), dma((2, 2, K, 2)),
            dma((2, 2, K, 2)), dma((2, 2, K, 2)),
            dma((2, NX, 2)), dma((2, NX, 2)),
        ],
        compiler_params=pltpu.CompilerParams(
            collective_id=0, has_side_effects=True, vmem_limit_bytes=50 * 1024 * 1024
        ),
    )(
        *(
            pltpu.with_memory_space_constraint(v, pltpu.HBM)
            for v in (routes.T, route_weight.T, tokens, cotangent, w_in[0], w_out[0])
        )
    )
    mixed, grad_tokens, grad_in, grad_out = pl.pallas_call(
        put_out,
        out_shape=tuple(jax.ShapeDtypeStruct(r.shape, r.dtype) for r in results),
        in_specs=[anywhere] * 4,
        out_specs=(pl.BlockSpec(memory_space=pltpu.HBM),) * 4,
        scratch_shapes=[dma((4,))],
        compiler_params=pltpu.CompilerParams(vmem_limit_bytes=1024 * 1024),
    )(*results)
    return mixed, grad_tokens, grad_in[None], grad_out[None]


def solution(mesh):
    placed = (
        P("expert", "dp"),
        P("expert", None),
        P("expert", None),
        P("expert", "dp"),
        P("expert", "dp", None),
        P("expert", None, "dp"),
    )
    return jax.shard_map(
        per_device,
        mesh=mesh,
        in_specs=placed,
        out_specs=(
            P("expert", "dp"),
            P("expert", "dp"),
            P("expert", "dp", None),
            P("expert", None, "dp"),
        ),
        check_vma=False,
    )
```
